32 devices in a mesh: dp: 4 (over y, x), seq: 8 (over z, core).
Axes of the slice: x: 2, y: 2, z: 4, core: 2. Of those that a mesh axis runs over, the one named last changes fastest.
Arguments:
- tokens: bfloat16 [4, 8192, 1152], P('dp', 'seq'), may hold values from -40 to 40
- d_out: bfloat16 [4, 8192, 1152], P('dp', 'seq'), may hold values from -6 to 6
- frames: int32 [4], P('dp'), may hold values from 16 to 32, as said below
- frame_order: int32 [4, 32], P('dp'), may hold values from 0 to 31, each once within a row
- w_qkv: bfloat16 [1152, 3456], replicated, may hold values from -4 to 4
- w_out: bfloat16 [1152, 1152], replicated, may hold values from -0.1875 to 0.1875
Outputs:
- d_tokens: bfloat16 [4, 8192, 1152], P('dp', 'seq')
- d_w_out: float32 [1152, 1152], P('seq', 'dp')
The draws below stay inside these ranges and needn't reach their ends.
Inputs may be any that keep to these rules, and one draw needn't show every extreme that they name: Some clip has 32 frames. `frame_order`: each row holds every number of 0 to 31 once.
All inputs are finite; a program needn't handle non-finite values.
Results may differ from the reference program's by a relative error of at most 0.012.
The reference program's roundings to bfloat16 on the way count: a program that leaves them out, or rounds other values in their place, can miss the bound.
Values may be sent and summed in bfloat16 or wider, within the bound.
A program may use at most 128 MiB of HBM per device.

```python
import math
import jax
import jax.numpy as jnp
from jax import lax

D = 1152
H = 16
P_SIZE = 256
F_MAX = 32
CLIPS = 1
CLIP_TOTAL = 4
ROWS = 8192
N_DP = 4


def draw_frames(key, part):
    clip_total = N_DP * CLIPS
    counts = jax.random.randint(jax.random.fold_in(key, 11), (clip_total,), F_MAX // 2, F_MAX + 1)
    largest_at = jax.random.randint(jax.random.fold_in(key, 12), (), 0, clip_total)
    return jnp.where(jnp.arange(clip_total) == largest_at, F_MAX, counts).astype(jnp.int32)


def draw_tokens(key, part):
    full_shape = (N_DP * CLIPS, F_MAX, P_SIZE, D)
    row_scales = jnp.exp(jax.random.uniform(jax.random.fold_in(key, 21), (N_DP * CLIPS, F_MAX, P_SIZE, 1), jnp.float32) * jnp.log(10.0))
    gaussian = jnp.clip(jax.random.normal(jax.random.fold_in(key, 23), full_shape, jnp.float32), -4.0, 4.0)
    result = gaussian * row_scales
    return result.reshape(N_DP * CLIPS, F_MAX * P_SIZE, D).astype(jnp.bfloat16)


def draw_w_qkv(key, part):
    matrix = jnp.clip(jax.random.normal(jax.random.fold_in(key, 31), (D, 3 * D), jnp.float32), -4.0, 4.0) * D ** (-0.5)
    return jnp.clip(matrix, -4.0, 4.0).astype(jnp.bfloat16)


def with_spikes(drawn, key, source, target, blocks, factor):
    owner, partner = [(jnp.arange(drawn.shape[dim]) // (drawn.shape[dim] // blocks)).reshape([-1 if axis == dim else 1 for axis in range(drawn.ndim)]) for dim in (source, target)]
    chosen = jax.random.permutation(key, blocks)[partner]
    strong = (owner == chosen) | (owner == (partner + blocks // 2) % blocks)
    return jnp.where(strong, factor * drawn, drawn)


def block_scale(stream_key, extent, shards, least, top_value):
    loudness = 1.0
    for axis_at, shards_of in shards:
        draws = jax.random.uniform(jax.random.fold_in(jax.random.fold_in(stream_key, 6), axis_at), (shards_of,), jnp.float32, least / len(shards), top_value / len(shards))
        loudness = loudness * jnp.repeat(jnp.exp(draws), extent[axis_at] // shards_of).reshape((-1,) + (1,) * (len(extent) - 1 - axis_at))
    return loudness


def bell_draw(own_key, dims, width, bound, split=(), held_as=jnp.bfloat16):
    entries = jax.random.normal(own_key, dims, jnp.float32) * width
    if len(split) > 0:
        entries = block_scale(own_key, dims, split, -0.22, 0.18) * entries
    return jnp.clip(entries, min=-bound, max=bound).astype(held_as)


def heavy_noise(key, dims, scale, reach, cuts, heavy, dtype=jnp.bfloat16):
    entries = scale * jax.random.normal(key, dims, jnp.float32)
    if cuts:
        entries = entries * block_scale(key, dims, cuts, -0.22, 0.18)
    return jnp.clip(with_spikes(entries, jax.random.fold_in(key, 3), *heavy), -reach, reach).astype(dtype)


def setup_inputs(seed: int = 0) -> dict:
    key_of = jax.random.split(jax.random.key(seed), 7)
    tokens = draw_tokens(jax.random.fold_in(key_of[6], 71), 0)
    d_out = heavy_noise(key_of[1], (CLIP_TOTAL, ROWS, D), 1.0, 6.0, ((0, 4), (1, 8)), (1, 2, 8, 2.0))
    frames = draw_frames(jax.random.fold_in(key_of[6], 71), 0)
    frame_order = jax.vmap(lambda own: jax.random.permutation(own, F_MAX))(jax.random.split(key_of[3], CLIP_TOTAL)).reshape((CLIP_TOTAL, F_MAX)).astype(jnp.int32)
    w_qkv = draw_w_qkv(jax.random.fold_in(key_of[6], 71), 0)
    w_out = bell_draw(key_of[5], (D, D), D ** -0.5, 0.1875)
    return dict(tokens=tokens, d_out=d_out, frames=frames, frame_order=frame_order, w_qkv=w_qkv, w_out=w_out)


def layer_stats(tokens):
    values = tokens.astype(jnp.float32)
    center = values - lax.optimization_barrier(jnp.mean(values, axis=-1, keepdims=True))
    spread = lax.optimization_barrier(jnp.mean(center * center, axis=-1, keepdims=True))
    inverse = lax.rsqrt(spread + 1e-06)
    return (center * inverse, inverse)

def attend_forward(queries, keys_in, values, live_slots, score_scale):
    scores = jnp.einsum('ciqhe,cjqhe->cqhij', queries.astype(jnp.float32), keys_in.astype(jnp.float32)) * score_scale
    scores = jnp.where(live_slots[:, None, None, None, :] > 0.5, scores, -1e+30)
    row_max = lax.optimization_barrier(jnp.max(scores, axis=-1, keepdims=True))
    exponent = jnp.exp(scores - row_max)
    softmax_out = exponent / lax.optimization_barrier(jnp.sum(exponent, axis=-1, keepdims=True))
    rounded = softmax_out.astype(jnp.bfloat16)
    attended = jnp.einsum('cqhij,cjqhe->ciqhe', rounded.astype(jnp.float32), values.astype(jnp.float32)).astype(jnp.bfloat16)
    return (softmax_out, rounded, attended)

def attend_backward(queries, keys_in, values, softmax_out, rounded, head_grad, score_scale):
    grad_float = head_grad.astype(jnp.float32)
    d_values = jnp.einsum('cqhij,ciqhe->cjqhe', rounded.astype(jnp.float32), grad_float).astype(jnp.bfloat16)
    prob_grad = jnp.einsum('ciqhe,cjqhe->cqhij', grad_float, values.astype(jnp.float32))
    inner_sum = lax.optimization_barrier(jnp.sum(softmax_out * prob_grad, axis=-1, keepdims=True))
    score_grad = (softmax_out * (prob_grad - inner_sum) * score_scale).astype(jnp.bfloat16)
    score_float = score_grad.astype(jnp.float32)
    d_queries = jnp.einsum('cqhij,cjqhe->ciqhe', score_float, keys_in.astype(jnp.float32)).astype(jnp.bfloat16)
    d_keys = jnp.einsum('cqhij,ciqhe->cjqhe', score_float, queries.astype(jnp.float32)).astype(jnp.bfloat16)
    return (d_queries, d_keys, d_values)

def reference(tokens, d_out, frames, frame_order, w_qkv, w_out):
    head_dim = D // H
    score_scale = 1.0 / math.sqrt(head_dim)
    grad_out = jnp.zeros((D, D), jnp.float32)
    results = []
    for clip_index in range(N_DP * CLIPS):
        live_slots = (frame_order[clip_index] < frames[clip_index]).astype(jnp.float32)
        row_live = jnp.repeat(live_slots, P_SIZE)
        normalized, inverse = layer_stats(tokens[clip_index])
        normed = normalized.astype(jnp.bfloat16)
        joined = jnp.dot(normed, w_qkv, preferred_element_type=jnp.float32).astype(jnp.bfloat16)
        head_grid = joined.reshape(1, F_MAX, P_SIZE, 3, H, head_dim)
        queries = head_grid[:, :, :, 0]
        keys_in = head_grid[:, :, :, 1]
        values = head_grid[:, :, :, 2]
        softmax_out, rounded, attended = attend_forward(queries, keys_in, values, live_slots[None, :], score_scale)
        masked = (d_out[clip_index].astype(jnp.float32) * row_live[:, None]).astype(jnp.bfloat16)
        head_rows = jnp.dot(masked, w_out.T, preferred_element_type=jnp.float32).astype(jnp.bfloat16)
        attended_rows = attended.reshape(F_MAX * P_SIZE, D)
        grad_out = grad_out + jnp.dot(attended_rows.T, masked, preferred_element_type=jnp.float32)
        head_grad = head_rows.reshape(1, F_MAX, P_SIZE, H, head_dim)
        d_queries, d_keys, d_values = attend_backward(queries, keys_in, values, softmax_out, rounded, head_grad, score_scale)
        qkv_grad = jnp.stack((d_queries, d_keys, d_values), axis=3).reshape(F_MAX * P_SIZE, 3 * D)
        normed_grad = jnp.dot(qkv_grad, w_qkv.T, preferred_element_type=jnp.float32)
        mean_grad = lax.optimization_barrier(jnp.mean(normed_grad, axis=-1, keepdims=True))
        mean_cross = lax.optimization_barrier(jnp.mean(normed_grad * normalized, axis=-1, keepdims=True))
        d_rows = masked.astype(jnp.float32) + inverse * (normed_grad - mean_grad - normalized * mean_cross)
        results.append(d_rows.astype(jnp.bfloat16))
    return (jnp.stack(results, axis=0), grad_out)
```

```python
import functools
import math

import jax
import jax.numpy as jnp
from jax import lax
from jax.experimental import pallas as pl
from jax.experimental.pallas import tpu as pltpu
from jax.sharding import PartitionSpec as P

H = 16
LANES = 128
GROUP = 8
NT = (((1,), (1,)), ((), ()))
TN = (((0,), (0,)), ((), ()))


def dot(a, b, dims=(((1,), (0,)), ((), ()))):
    return lax.dot_general(a, b, dims, preferred_element_type=jnp.float32)


def attend(joined, head_grad, mask, attended, qkv_grad, width, score_scale):
    head_dim = width // H
    column = lax.broadcasted_iota(jnp.int32, (1, 2 * LANES), 1)
    pending = [{}, {}, {}, {}]
    for h in range(H):
        low, high = h * head_dim, (h + 1) * head_dim
        first, last = low // LANES, -(-high // LANES)
        start, size = first * LANES, (last - first) * LANES
        keep = jnp.where(
            (column[:, :size] >= low - start) & (column[:, :size] < high - start), 1.0, 0.0
        ).astype(jnp.bfloat16)
        q = joined[:, start : start + size] * keep
        k = joined[:, width + start : width + start + size] * keep
        v = joined[:, 2 * width + start : 2 * width + start + size] * keep
        g = head_grad[:, start : start + size] * keep
        scores = dot(q, k, NT) * score_scale + mask
        exponent = jnp.exp(scores - jnp.max(scores, axis=-1, keepdims=True))
        probs = exponent * (1.0 / jnp.sum(exponent, axis=-1, keepdims=True))
        rounded = probs.astype(jnp.bfloat16)
        prob_grad = dot(g, v, NT)
        inner = jnp.sum(probs * prob_grad, axis=-1, keepdims=True)
        score_grad = (probs * (prob_grad - inner) * score_scale).astype(jnp.bfloat16)
        results = (
            dot(rounded, v),
            dot(score_grad, k),
            dot(score_grad, q, TN),
            dot(rounded, g, TN),
        )
        for which, result in enumerate(results):
            for tile in range(first, last):
                piece = result[:, (tile - first) * LANES : (tile - first + 1) * LANES]
                held = pending[which].pop(tile, None)
                piece = piece if held is None else held + piece
                if (tile + 1) * LANES <= high:
                    piece = piece.astype(jnp.bfloat16)
                    if which == 0:
                        attended[:, tile * LANES : (tile + 1) * LANES] = piece
                    else:
                        at = (which - 1) * width + tile * LANES
                        qkv_grad[:, at : at + LANES] = piece
                else:
                    pending[which][tile] = piece


def kernel(
    score_scale,
    tokens_ref,
    d_out_ref,
    live_ref,
    mask_ref,
    w_qkv_ref,
    w_out_ref,
    d_tokens_ref,
    grad_ref,
    joined,
    head_grad,
    attended,
    qkv_grad,
):
    rows, width = attended.shape
    values = tokens_ref[...].astype(jnp.float32).reshape(rows, width)
    center = values - jnp.mean(values, axis=-1, keepdims=True)
    inverse = lax.rsqrt(jnp.mean(center * center, axis=-1, keepdims=True) + 1e-06)
    normalized = center * inverse
    normed = normalized.astype(jnp.bfloat16)
    masked_wide = d_out_ref[...].astype(jnp.float32).reshape(rows, width) * live_ref[...]
    masked = masked_wide.astype(jnp.bfloat16)
    joined[...] = dot(normed, w_qkv_ref[...]).astype(jnp.bfloat16)
    head_grad[...] = dot(masked, w_out_ref[...], NT).astype(jnp.bfloat16)
    attend(joined, head_grad, mask_ref[...], attended, qkv_grad, width, score_scale)
    term = dot(attended[...], masked, TN)

    @pl.when(pl.program_id(0) == 0)
    def _():
        grad_ref[...] = term

    @pl.when(pl.program_id(0) != 0)
    def _():
        grad_ref[...] += term

    normed_grad = dot(qkv_grad[...], w_qkv_ref[...], NT)
    mean_grad = jnp.mean(normed_grad, axis=-1, keepdims=True)
    mean_cross = jnp.mean(normed_grad * normalized, axis=-1, keepdims=True)
    result = masked_wide + inverse * (normed_grad - mean_grad - normalized * mean_cross)
    d_tokens_ref[...] = result.reshape(d_tokens_ref.shape).astype(jnp.bfloat16)


def local_part(tokens, d_out, live_slots, w_qkv, w_out):
    slot_count, stripe, width = tokens.shape
    group = min(GROUP, stripe)
    rows = slot_count * group
    steps = stripe // group
    at = jnp.arange(rows, dtype=jnp.int32)
    live_rows = jnp.repeat(live_slots, group)
    mask = jnp.where(
        (at[:, None] % group == at[None, :] % group) & (live_rows[None, :] > 0.5), 0.0, -1e30
    ).astype(jnp.float32)
    if steps == 1:
        tokens, d_out = tokens.reshape(rows, width), d_out.reshape(rows, width)
        moving = pl.BlockSpec((rows, width), lambda i: (0, 0))
    else:
        moving = pl.BlockSpec((slot_count, group, width), lambda i: (0, i, 0))

    def whole(shape):
        return pl.BlockSpec(shape, lambda i: (0, 0), pipeline_mode=pl.Buffered(1))

    d_tokens, grad = pl.pallas_call(
        functools.partial(kernel, 1.0 / math.sqrt(width // H)),
        grid=(steps,),
        in_specs=[
            moving,
            moving,
            whole((rows, 1)),
            whole((rows, rows)),
            whole(w_qkv.shape),
            whole(w_out.shape),
        ],
        out_specs=[moving, whole((width, width))],
        out_shape=[
            jax.ShapeDtypeStruct(tokens.shape, jnp.bfloat16),
            jax.ShapeDtypeStruct((width, width), jnp.float32),
        ],
        scratch_shapes=[
            pltpu.VMEM((rows, 3 * width), jnp.bfloat16),
            pltpu.VMEM((rows, width), jnp.bfloat16),
            pltpu.VMEM((rows, width), jnp.bfloat16),
            pltpu.VMEM((rows, 3 * width), jnp.bfloat16),
        ],
        compiler_params=pltpu.CompilerParams(
            dimension_semantics=("arbitrary",), vmem_limit_bytes=60 * 2**20
        ),
    )(tokens, d_out, live_rows[:, None], mask, w_qkv, w_out)
    return d_tokens.reshape(slot_count, stripe, width), grad


def body(tokens, d_out, frames, frame_order, w_qkv, w_out):
    _, row_count, width = tokens.shape
    seq_size = lax.axis_size("seq")
    slot_count = frame_order.shape[1]
    stripe = row_count // slot_count
    patch_count = row_count * seq_size // slot_count
    slots = max(1, row_count // patch_count)
    piece = row_count // slots // seq_size
    live_slots = (frame_order[0] < frames[0]).astype(jnp.float32)

    def spread(rows):
        sent = rows.reshape(slots, seq_size, piece, width)
        got = lax.all_to_all(sent, "seq", split_axis=1, concat_axis=0, tiled=True)
        return got.reshape(slot_count, stripe, width)

    d_rows, grad_out = local_part(spread(tokens), spread(d_out), live_slots, w_qkv, w_out)
    back = d_rows.reshape(seq_size * slots, 1, piece, width)
    d_tokens = lax.all_to_all(back, "seq", split_axis=0, concat_axis=1, tiled=True)
    share = lax.psum_scatter(
        grad_out.astype(jnp.bfloat16), "dp", scatter_dimension=1, tiled=True
    ).astype(jnp.float32)
    final_out = lax.psum_scatter(share, "seq", scatter_dimension=0, tiled=True)
    return (d_tokens.reshape(tokens.shape), final_out)


def solution(mesh):
    placed = (P("dp", "seq", None), P("dp", "seq", None), P("dp"), P("dp", None), P(), P())
    return jax.shard_map(
        body,
        mesh=mesh,
        in_specs=placed,
        out_specs=(P("dp", "seq", None), P("seq", "dp")),
        check_vma=False,
    )
```

```python
import functools
import math

import jax
import jax.numpy as jnp
from jax import lax
from jax.experimental import pallas as pl
from jax.experimental.pallas import tpu as pltpu
from jax.sharding import PartitionSpec as P

H = 16
LANES = 128
GROUP = 8
NT = (((1,), (1,)), ((), ()))
TN = (((0,), (0,)), ((), ()))


def dot(a, b, dims=(((1,), (0,)), ((), ()))):
    return lax.dot_general(a, b, dims, preferred_element_type=jnp.float32)


def attend(joined, head_grad, mask, attended, qkv_grad, width, score_scale):
    head_dim = width // H
    column = lax.broadcasted_iota(jnp.int32, (1, 2 * LANES), 1)
    pending = [{}, {}, {}, {}]
    for h in range(H):
        low, high = h * head_dim, (h + 1) * head_dim
        first, last = low // LANES, -(-high // LANES)
        start, size = first * LANES, (last - first) * LANES
        keep = jnp.where(
            (column[:, :size] >= low - start) & (column[:, :size] < high - start), 1.0, 0.0
        ).astype(jnp.bfloat16)
        q = joined[:, start : start + size] * keep
        k = joined[:, width + start : width + start + size] * keep
        v = joined[:, 2 * width + start : 2 * width + start + size] * keep
        g = head_grad[:, start : start + size] * keep
        scores = dot(q, k, NT) * score_scale + mask
        exponent = jnp.exp(scores - jnp.max(scores, axis=-1, keepdims=True))
        probs = exponent * (1.0 / jnp.sum(exponent, axis=-1, keepdims=True))
        rounded = probs.astype(jnp.bfloat16)
        prob_grad = dot(g, v, NT)
        inner = jnp.sum(probs * prob_grad, axis=-1, keepdims=True)
        score_grad = (probs * (prob_grad - inner) * score_scale).astype(jnp.bfloat16)
        results = (
            dot(rounded, v),
            dot(score_grad, k),
            dot(score_grad, q, TN),
            dot(rounded, g, TN),
        )
        for which, result in enumerate(results):
            for tile in range(first, last):
                piece = result[:, (tile - first) * LANES : (tile - first + 1) * LANES]
                held = pending[which].pop(tile, None)
                piece = piece if held is None else held + piece
                if (tile + 1) * LANES <= high:
                    piece = piece.astype(jnp.bfloat16)
                    if which == 0:
                        attended[:, tile * LANES : (tile + 1) * LANES] = piece
                    else:
                        at = (which - 1) * width + tile * LANES
                        qkv_grad[:, at : at + LANES] = piece
                else:
                    pending[which][tile] = piece


def kernel(
    score_scale,
    tokens_ref,
    d_out_ref,
    live_ref,
    mask_ref,
    w_qkv_ref,
    w_out_ref,
    d_tokens_ref,
    grad_ref,
    joined,
    head_grad,
    attended,
    qkv_grad,
):
    rows, width = attended.shape
    values = tokens_ref[...].astype(jnp.float32).reshape(rows, width)
    center = values - jnp.mean(values, axis=-1, keepdims=True)
    inverse = lax.rsqrt(jnp.mean(center * center, axis=-1, keepdims=True) + 1e-06)
    normalized = center * inverse
    normed = normalized.astype(jnp.bfloat16)
    masked_wide = d_out_ref[...].astype(jnp.float32).reshape(rows, width) * live_ref[...]
    masked = masked_wide.astype(jnp.bfloat16)
    joined[...] = dot(normed, w_qkv_ref[...]).astype(jnp.bfloat16)
    head_grad[...] = dot(masked, w_out_ref[...], NT).astype(jnp.bfloat16)
    attend(joined, head_grad, mask_ref[...], attended, qkv_grad, width, score_scale)
    term = dot(attended[...], masked, TN)

    @pl.when(pl.program_id(0) == 0)
    def _():
        grad_ref[...] = term

    @pl.when(pl.program_id(0) != 0)
    def _():
        grad_ref[...] += term

    normed_grad = dot(qkv_grad[...], w_qkv_ref[...], NT)
    mean_grad = jnp.mean(normed_grad, axis=-1, keepdims=True)
    mean_cross = jnp.mean(normed_grad * normalized, axis=-1, keepdims=True)
    result = masked_wide + inverse * (normed_grad - mean_grad - normalized * mean_cross)
    d_tokens_ref[...] = result.reshape(d_tokens_ref.shape).astype(jnp.bfloat16)


def mask_of(live_slots, rows, group):
    at = jnp.arange(rows, dtype=jnp.int32)
    live_rows = jnp.repeat(live_slots, group)
    mask = jnp.where(
        (at[:, None] % group == at[None, :] % group) & (live_rows[None, :] > 0.5), 0.0, -1e30
    ).astype(jnp.float32)
    return live_rows, mask


def local_part(tokens, d_out, live_slots, w_qkv, w_out):
    slot_count, stripe, width = tokens.shape
    group = min(GROUP, stripe)
    rows = slot_count * group
    steps = stripe // group
    live_rows, mask = mask_of(live_slots, rows, group)
    if steps == 1:
        tokens, d_out = tokens.reshape(rows, width), d_out.reshape(rows, width)
        moving = pl.BlockSpec((rows, width), lambda i: (0, 0))
    else:
        moving = pl.BlockSpec((slot_count, group, width), lambda i: (0, i, 0))

    def whole(shape):
        return pl.BlockSpec(shape, lambda i: (0, 0), pipeline_mode=pl.Buffered(1))

    d_tokens, grad = pl.pallas_call(
        functools.partial(kernel, 1.0 / math.sqrt(width // H)),
        grid=(steps,),
        in_specs=[
            moving,
            moving,
            whole((rows, 1)),
            whole((rows, rows)),
            whole(w_qkv.shape),
            whole(w_out.shape),
        ],
        out_specs=[moving, whole((width, width))],
        out_shape=[
            jax.ShapeDtypeStruct(tokens.shape, jnp.bfloat16),
            jax.ShapeDtypeStruct((width, width), jnp.float32),
        ],
        scratch_shapes=[
            pltpu.VMEM((rows, 3 * width), jnp.bfloat16),
            pltpu.VMEM((rows, width), jnp.bfloat16),
            pltpu.VMEM((rows, width), jnp.bfloat16),
            pltpu.VMEM((rows, 3 * width), jnp.bfloat16),
        ],
        compiler_params=pltpu.CompilerParams(
            dimension_semantics=("arbitrary",), vmem_limit_bytes=60 * 2**20
        ),
    )(tokens, d_out, live_rows[:, None], mask, w_qkv, w_out)
    return d_tokens.reshape(slot_count, stripe, width), grad


def exchange_kernel(
    score_scale,
    seq_size,
    dp_size,
    tokens_ref,
    d_out_ref,
    live_ref,
    mask_ref,
    w_qkv_hbm,
    w_out_hbm,
    d_tokens_ref,
    final_ref,
    w_qkv_ref,
    w_out_ref,
    got_tokens,
    got_d_out,
    results,
    joined,
    head_grad,
    attended,
    qkv_grad,
    grad,
    pair_sent,
    pair_got,
    dp_sent,
    dp_got,
    chip_sent,
    chip_got,
    weight_sems,
    tokens_send,
    tokens_recv,
    d_out_send,
    d_out_recv,
    back_send,
    back_recv,
    pair_sems,
    dp_send,
    dp_recv,
    chip_send,
    chip_recv,
):
    rows, width = attended.shape
    steps, slot_count, group, _ = got_tokens.shape
    slots = tokens_ref.shape[0]
    stripe = steps * group
    chips = seq_size // 2
    row_block, column_block = final_ref.shape
    me = lax.axis_index("seq")
    my_dp = lax.axis_index("dp")
    core = lax.rem(me, 2)
    chip = me // 2

    def peer(k):
        return lax.rem(me + k, seq_size)

    def dp_peer(k):
        return lax.rem(my_dp + k, dp_size)

    barrier = pltpu.get_barrier_semaphore()
    for k in range(1, seq_size):
        pl.semaphore_signal(
            barrier,
            inc=1,
            device_id={"seq": peer(k)},
            device_id_type=pl.DeviceIdType.MESH,
        )
    for k in range(1, dp_size):
        pl.semaphore_signal(
            barrier,
            inc=1,
            device_id={"dp": dp_peer(k)},
            device_id_type=pl.DeviceIdType.MESH,
        )
    weights = (
        pltpu.make_async_copy(w_qkv_hbm, w_qkv_ref, weight_sems.at[0]),
        pltpu.make_async_copy(w_out_hbm, w_out_ref, weight_sems.at[1]),
    )
    for copy in weights:
        copy.start()
    pl.semaphore_wait(barrier, seq_size - 1 + dp_size - 1)

    def remote(source, target, send, recv, device):
        return pltpu.make_async_remote_copy(
            src_ref=source,
            dst_ref=target,
            send_sem=send,
            recv_sem=recv,
            device_id=device,
            device_id_type=pl.DeviceIdType.MESH,
        )

    def home(ref, owner, g):
        return ref.at[:, pl.ds(pl.multiple_of(owner * stripe + g * group, group), group), :]

    def away(ref, owner, g):
        return ref.at[g, pl.ds(owner * slots, slots)]

    def spread(source, target, send, recv, g, k):
        return remote(
            home(source, peer(k), g),
            away(target, me, g),
            send.at[g, k],
            recv.at[g, k],
            {"seq": peer(k)},
        )

    def keep_own(source, target, recv, g):
        return pltpu.make_async_copy(home(source, me, g), away(target, me, g), recv.at[g, 0])

    def back(g, k):
        return remote(
            away(results, peer(k), g),
            home(d_tokens_ref, me, g),
            back_send.at[g, k],
            back_recv.at[g, k],
            {"seq": peer(k)},
        )

    def back_own(g):
        return pltpu.make_async_copy(
            away(results, me, g), home(d_tokens_ref, me, g), back_recv.at[g, 0]
        )

    moved = (
        (tokens_ref, got_tokens, tokens_send, tokens_recv),
        (d_out_ref, got_d_out, d_out_send, d_out_recv),
    )

    @pl.loop(0, steps)
    def _(g):
        for source, target, send, recv in moved:
            for k in range(1, seq_size):
                spread(source, target, send, recv, g, k).start()
            keep_own(source, target, recv, g).start()

    def arrived(which, g):
        source, target, send, recv = moved[which]
        for k in range(1, seq_size):
            spread(source, target, send, recv, g, k).wait_recv()
        keep_own(source, target, recv, g).wait()

    for copy in weights:
        copy.wait()
    grad[...] = jnp.zeros_like(grad)

    def pair_copy():
        return remote(
            pair_sent, pair_got, pair_sems.at[0], pair_sems.at[1], {"seq": chip * 2 + 1 - core}
        )

    def row_piece(at, parity):
        start = pl.multiple_of((at * 2 + parity) * row_block, row_block)
        return grad[pl.ds(start, row_block), :]

    def columns_of(value, d):
        return value[:, d * column_block : (d + 1) * column_block]

    @pl.loop(0, steps)
    def _(g):
        arrived(0, g)
        values = got_tokens[g].astype(jnp.float32).reshape(rows, width)
        center = values - jnp.mean(values, axis=-1, keepdims=True)
        inverse = lax.rsqrt(jnp.mean(center * center, axis=-1, keepdims=True) + 1e-06)
        normalized = center * inverse
        joined[...] = dot(normalized.astype(jnp.bfloat16), w_qkv_ref[...]).astype(jnp.bfloat16)
        arrived(1, g)
        masked_wide = got_d_out[g].astype(jnp.float32).reshape(rows, width) * live_ref[...]
        masked = masked_wide.astype(jnp.bfloat16)
        head_grad[...] = dot(masked, w_out_ref[...], NT).astype(jnp.bfloat16)
        attend(joined, head_grad, mask_ref[...], attended, qkv_grad, width, score_scale)
        grad[...] += dot(attended[...], masked, TN)

        @pl.when(g == steps - 1)
        def _():
            @pl.loop(0, chips)
            def _(at):
                value = row_piece(at, 1 - core)
                for d in range(dp_size):
                    pair_sent[d, at] = columns_of(value, d).astype(jnp.bfloat16)

            pair_copy().start()

        normed_grad = dot(qkv_grad[...], w_qkv_ref[...], NT)
        mean_grad = jnp.mean(normed_grad, axis=-1, keepdims=True)
        mean_cross = jnp.mean(normed_grad * normalized, axis=-1, keepdims=True)
        result = masked_wide + inverse * (normed_grad - mean_grad - normalized * mean_cross)
        results[g] = result.reshape(slot_count, group, width).astype(jnp.bfloat16)
        for k in range(1, seq_size):
            back(g, k).start()
        back_own(g).start()

    pair_copy().wait_recv()

    @pl.loop(0, chips)
    def _(at):
        value = row_piece(at, core)
        for d in range(dp_size):
            total = columns_of(value, d) + pair_got[d, at].astype(jnp.float32)
            dp_sent[d, at] = total.astype(jnp.bfloat16)

    def dp_copy(k):
        return remote(
            dp_sent.at[dp_peer(k)],
            dp_got.at[k - 1],
            dp_send.at[k - 1],
            dp_recv.at[k - 1],
            {"dp": dp_peer(k)},
        )

    for k in range(1, dp_size):
        dp_copy(k).start()
    for k in range(1, dp_size):
        dp_copy(k).wait_recv()

    @pl.loop(0, chips)
    def _(at):
        total = dp_sent[my_dp, at].astype(jnp.float32)
        for k in range(1, dp_size):
            total = total + dp_got[k - 1, at].astype(jnp.float32)
        chip_sent[at] = total.astype(jnp.bfloat16)

    def chip_copy(k):
        target = lax.rem(chip + k, chips)
        return remote(
            chip_sent.at[target],
            chip_got.at[k - 1],
            chip_send.at[k - 1],
            chip_recv.at[k - 1],
            {"seq": target * 2 + core},
        )

    for k in range(1, chips):
        chip_copy(k).start()
    total = chip_sent[chip].astype(jnp.float32)
    for k in range(1, chips):
        chip_copy(k).wait_recv()
        total = total + chip_got[k - 1].astype(jnp.float32)
    final_ref[...] = total

    pair_copy().wait_send()
    for k in range(1, dp_size):
        dp_copy(k).wait_send()
    for k in range(1, chips):
        chip_copy(k).wait_send()

    @pl.loop(0, steps)
    def _(g):
        for source, target, send, recv in moved:
            for k in range(1, seq_size):
                spread(source, target, send, recv, g, k).wait_send()
        for k in range(1, seq_size):
            back(g, k).wait()
        back_own(g).wait()


def exchange_part(tokens, d_out, live_slots, w_qkv, w_out, slots, seq_size, dp_size):
    row_count, width = tokens.shape
    slot_count = live_slots.shape[0]
    stripe = row_count // slot_count
    steps = stripe // GROUP
    rows = slot_count * GROUP
    chips = seq_size // 2
    live_rows, mask = mask_of(live_slots, rows, GROUP)
    tokens = tokens.reshape(slots, row_count // slots, width)
    d_out = d_out.reshape(tokens.shape)
    any_space = pl.BlockSpec(memory_space=pl.ANY)
    vmem = pl.BlockSpec(memory_space=pltpu.VMEM)
    narrow = jnp.bfloat16
    parts = (chips, width // seq_size, width // dp_size)
    crossing = pltpu.SemaphoreType.DMA((steps, seq_size))
    d_tokens, final = pl.pallas_call(
        functools.partial(exchange_kernel, 1.0 / math.sqrt(width // H), seq_size, dp_size),
        in_specs=[any_space, any_space, vmem, vmem, any_space, any_space],
        out_specs=[any_space, vmem],
        out_shape=[
            jax.ShapeDtypeStruct(tokens.shape, narrow),
            jax.ShapeDtypeStruct(parts[1:], jnp.float32),
        ],
        scratch_shapes=[
            pltpu.VMEM(w_qkv.shape, narrow),
            pltpu.VMEM(w_out.shape, narrow),
            pltpu.VMEM((steps, slot_count, GROUP, width), narrow),
            pltpu.VMEM((steps, slot_count, GROUP, width), narrow),
            pltpu.VMEM((steps, slot_count, GROUP, width), narrow),
            pltpu.VMEM((rows, 3 * width), narrow),
            pltpu.VMEM((rows, width), narrow),
            pltpu.VMEM((rows, width), narrow),
            pltpu.VMEM((rows, 3 * width), narrow),
            pltpu.VMEM((width, width), jnp.float32),
            pltpu.VMEM((dp_size, *parts), narrow),
            pltpu.VMEM((dp_size, *parts), narrow),
            pltpu.VMEM((dp_size, *parts), narrow),
            pltpu.VMEM((dp_size - 1, *parts), narrow),
            pltpu.VMEM(parts, narrow),
            pltpu.VMEM((chips - 1, *parts[1:]), narrow),
            pltpu.SemaphoreType.DMA((2,)),
            crossing,
            crossing,
            crossing,
            crossing,
            crossing,
            crossing,
            pltpu.SemaphoreType.DMA((2,)),
            pltpu.SemaphoreType.DMA((dp_size - 1,)),
            pltpu.SemaphoreType.DMA((dp_size - 1,)),
            pltpu.SemaphoreType.DMA((chips - 1,)),
            pltpu.SemaphoreType.DMA((chips - 1,)),
        ],
        compiler_params=pltpu.CompilerParams(
            collective_id=0, has_side_effects=True, vmem_limit_bytes=60 * 2**20
        ),
    )(tokens, d_out, live_rows[:, None], mask, w_qkv, w_out)
    return d_tokens, final


def body(tokens, d_out, frames, frame_order, w_qkv, w_out):
    _, row_count, width = tokens.shape
    seq_size = lax.axis_size("seq")
    slot_count = frame_order.shape[1]
    stripe = row_count // slot_count
    patch_count = row_count * seq_size // slot_count
    slots = max(1, row_count // patch_count)
    piece = row_count // slots // seq_size
    live_slots = (frame_order[0] < frames[0]).astype(jnp.float32)

    dp_size = lax.axis_size("dp")
    if (
        piece == stripe
        and stripe % GROUP == 0
        and seq_size % 2 == 0
        and seq_size > 2
        and dp_size > 1
        and width % (16 * seq_size) == 0
    ):
        d_rows, final_out = exchange_part(
            tokens[0], d_out[0], live_slots, w_qkv, w_out, slots, seq_size, dp_size
        )
        return (d_rows.reshape(tokens.shape), final_out)

    def spread(rows):
        sent = rows.reshape(slots, seq_size, piece, width)
        got = lax.all_to_all(sent, "seq", split_axis=1, concat_axis=0, tiled=True)
        return got.reshape(slot_count, stripe, width)

    d_rows, grad_out = local_part(spread(tokens), spread(d_out), live_slots, w_qkv, w_out)
    back = d_rows.reshape(seq_size * slots, 1, piece, width)
    d_tokens = lax.all_to_all(back, "seq", split_axis=0, concat_axis=1, tiled=True)
    share = lax.psum_scatter(
        grad_out.astype(jnp.bfloat16), "dp", scatter_dimension=1, tiled=True
    ).astype(jnp.float32)
    final_out = lax.psum_scatter(share, "seq", scatter_dimension=0, tiled=True)
    return (d_tokens.reshape(tokens.shape), final_out)


def solution(mesh):
    placed = (P("dp", "seq", None), P("dp", "seq", None), P("dp"), P("dp", None), P(), P())
    return jax.shard_map(
        body,
        mesh=mesh,
        in_specs=placed,
        out_specs=(P("dp", "seq", None), P("seq", "dp")),
        check_vma=False,
    )
```

```python
import functools
import math

import jax
import jax.numpy as jnp
from jax import lax
from jax.experimental import pallas as pl
from jax.experimental.pallas import tpu as pltpu
from jax.sharding import PartitionSpec as P

H = 16
LANES = 128
GROUP = 8
NT = (((1,), (1,)), ((), ()))
TN = (((0,), (0,)), ((), ()))


def dot(a, b, dims=(((1,), (0,)), ((), ()))):
    return lax.dot_general(a, b, dims, preferred_element_type=jnp.float32)


def attend(joined, head_grad, mask, attended, qkv_grad, width, score_scale):
    head_dim = width // H
    column = lax.broadcasted_iota(jnp.int32, (1, 2 * LANES), 1)
    pending = [{}, {}, {}, {}]
    for h in range(H):
        low, high = h * head_dim, (h + 1) * head_dim
        first, last = low // LANES, -(-high // LANES)
        start, size = first * LANES, (last - first) * LANES
        keep = jnp.where(
            (column[:, :size] >= low - start) & (column[:, :size] < high - start), 1.0, 0.0
        ).astype(jnp.bfloat16)
        q = joined[:, start : start + size] * keep
        k = joined[:, width + start : width + start + size] * keep
        v = joined[:, 2 * width + start : 2 * width + start + size] * keep
        g = head_grad[:, start : start + size] * keep
        scores = dot(q, k, NT) * score_scale + mask
        exponent = jnp.exp(scores - jnp.max(scores, axis=-1, keepdims=True))
        probs = exponent * (1.0 / jnp.sum(exponent, axis=-1, keepdims=True))
        rounded = probs.astype(jnp.bfloat16)
        prob_grad = dot(g, v, NT)
        inner = jnp.sum(probs * prob_grad, axis=-1, keepdims=True)
        score_grad = (probs * (prob_grad - inner) * score_scale).astype(jnp.bfloat16)
        results = (
            dot(rounded, v),
            dot(score_grad, k),
            dot(score_grad, q, TN),
            dot(rounded, g, TN),
        )
        for which, result in enumerate(results):
            for tile in range(first, last):
                piece = result[:, (tile - first) * LANES : (tile - first + 1) * LANES]
                held = pending[which].pop(tile, None)
                piece = piece if held is None else held + piece
                if (tile + 1) * LANES <= high:
                    piece = piece.astype(jnp.bfloat16)
                    if which == 0:
                        attended[:, tile * LANES : (tile + 1) * LANES] = piece
                    else:
                        at = (which - 1) * width + tile * LANES
                        qkv_grad[:, at : at + LANES] = piece
                else:
                    pending[which][tile] = piece


def kernel(
    score_scale,
    tokens_ref,
    d_out_ref,
    live_ref,
    mask_ref,
    w_qkv_ref,
    w_out_ref,
    d_tokens_ref,
    grad_ref,
    joined,
    head_grad,
    attended,
    qkv_grad,
):
    rows, width = attended.shape
    values = tokens_ref[...].astype(jnp.float32).reshape(rows, width)
    center = values - jnp.mean(values, axis=-1, keepdims=True)
    inverse = lax.rsqrt(jnp.mean(center * center, axis=-1, keepdims=True) + 1e-06)
    normalized = center * inverse
    normed = normalized.astype(jnp.bfloat16)
    masked_wide = d_out_ref[...].astype(jnp.float32).reshape(rows, width) * live_ref[...]
    masked = masked_wide.astype(jnp.bfloat16)
    joined[...] = dot(normed, w_qkv_ref[...]).astype(jnp.bfloat16)
    head_grad[...] = dot(masked, w_out_ref[...], NT).astype(jnp.bfloat16)
    attend(joined, head_grad, mask_ref[...], attended, qkv_grad, width, score_scale)
    term = dot(attended[...], masked, TN)

    @pl.when(pl.program_id(0) == 0)
    def _():
        grad_ref[...] = term

    @pl.when(pl.program_id(0) != 0)
    def _():
        grad_ref[...] += term

    normed_grad = dot(qkv_grad[...], w_qkv_ref[...], NT)
    mean_grad = jnp.mean(normed_grad, axis=-1, keepdims=True)
    mean_cross = jnp.mean(normed_grad * normalized, axis=-1, keepdims=True)
    result = masked_wide + inverse * (normed_grad - mean_grad - normalized * mean_cross)
    d_tokens_ref[...] = result.reshape(d_tokens_ref.shape).astype(jnp.bfloat16)


def mask_of(live_slots, rows, group):
    at = jnp.arange(rows, dtype=jnp.int32)
    live_rows = jnp.repeat(live_slots, group)
    mask = jnp.where(
        (at[:, None] % group == at[None, :] % group) & (live_rows[None, :] > 0.5), 0.0, -1e30
    ).astype(jnp.float32)
    return live_rows, mask


def local_part(tokens, d_out, live_slots, w_qkv, w_out):
    slot_count, stripe, width = tokens.shape
    group = min(GROUP, stripe)
    rows = slot_count * group
    steps = stripe // group
    live_rows, mask = mask_of(live_slots, rows, group)
    if steps == 1:
        tokens, d_out = tokens.reshape(rows, width), d_out.reshape(rows, width)
        moving = pl.BlockSpec((rows, width), lambda i: (0, 0))
    else:
        moving = pl.BlockSpec((slot_count, group, width), lambda i: (0, i, 0))

    def whole(shape):
        return pl.BlockSpec(shape, lambda i: (0, 0), pipeline_mode=pl.Buffered(1))

    d_tokens, grad = pl.pallas_call(
        functools.partial(kernel, 1.0 / math.sqrt(width // H)),
        grid=(steps,),
        in_specs=[
            moving,
            moving,
            whole((rows, 1)),
            whole((rows, rows)),
            whole(w_qkv.shape),
            whole(w_out.shape),
        ],
        out_specs=[moving, whole((width, width))],
        out_shape=[
            jax.ShapeDtypeStruct(tokens.shape, jnp.bfloat16),
            jax.ShapeDtypeStruct((width, width), jnp.float32),
        ],
        scratch_shapes=[
            pltpu.VMEM((rows, 3 * width), jnp.bfloat16),
            pltpu.VMEM((rows, width), jnp.bfloat16),
            pltpu.VMEM((rows, width), jnp.bfloat16),
            pltpu.VMEM((rows, 3 * width), jnp.bfloat16),
        ],
        compiler_params=pltpu.CompilerParams(
            dimension_semantics=("arbitrary",), vmem_limit_bytes=60 * 2**20
        ),
    )(tokens, d_out, live_rows[:, None], mask, w_qkv, w_out)
    return d_tokens.reshape(slot_count, stripe, width), grad


def exchange_kernel(
    score_scale,
    seq_size,
    dp_size,
    tokens_ref,
    d_out_ref,
    frames_ref,
    order_ref,
    w_qkv_hbm,
    w_out_hbm,
    d_tokens_ref,
    final_ref,
    w_qkv_ref,
    w_out_ref,
    got_tokens,
    got_d_out,
    results,
    joined,
    head_grad,
    attended,
    qkv_grad,
    grad,
    pair_sent,
    pair_got,
    dp_sent,
    dp_got,
    chip_sent,
    chip_got,
    live_ref,
    mask_ref,
    weight_sems,
    tokens_send,
    tokens_recv,
    d_out_send,
    d_out_recv,
    back_send,
    back_recv,
    pair_sems,
    dp_send,
    dp_recv,
    chip_send,
    chip_recv,
):
    rows, width = attended.shape
    steps, slot_count, group, _ = got_tokens.shape
    slots = tokens_ref.shape[0]
    stripe = steps * group
    chips = seq_size // 2
    row_block, column_block = final_ref.shape
    me = lax.axis_index("seq")
    my_dp = lax.axis_index("dp")
    core = lax.rem(me, 2)
    chip = me // 2

    def peer(k):
        return lax.rem(me + k, seq_size)

    def dp_peer(k):
        return lax.rem(my_dp + k, dp_size)

    barrier = pltpu.get_barrier_semaphore()
    for k in range(1, seq_size):
        pl.semaphore_signal(
            barrier,
            inc=1,
            device_id={"seq": peer(k)},
            device_id_type=pl.DeviceIdType.MESH,
        )
    for k in range(1, dp_size):
        pl.semaphore_signal(
            barrier,
            inc=1,
            device_id={"dp": dp_peer(k)},
            device_id_type=pl.DeviceIdType.MESH,
        )
    weights = (
        pltpu.make_async_copy(w_qkv_hbm, w_qkv_ref, weight_sems.at[0]),
        pltpu.make_async_copy(w_out_hbm, w_out_ref, weight_sems.at[1]),
    )
    for copy in weights:
        copy.start()
    pl.semaphore_wait(barrier, seq_size - 1 + dp_size - 1)

    def remote(source, target, send, recv, device):
        return pltpu.make_async_remote_copy(
            src_ref=source,
            dst_ref=target,
            send_sem=send,
            recv_sem=recv,
            device_id=device,
            device_id_type=pl.DeviceIdType.MESH,
        )

    def home(ref, owner, g):
        return ref.at[:, pl.ds(pl.multiple_of(owner * stripe + g * group, group), group), :]

    def away(ref, owner, g):
        return ref.at[g, pl.ds(owner * slots, slots)]

    def spread(source, target, send, recv, g, k):
        return remote(
            home(source, peer(k), g),
            away(target, me, g),
            send.at[g, k],
            recv.at[g, k],
            {"seq": peer(k)},
        )

    def keep_own(source, target, recv, g):
        return pltpu.make_async_copy(home(source, me, g), away(target, me, g), recv.at[g, 0])

    def back(g, k):
        return remote(
            away(results, peer(k), g),
            home(d_tokens_ref, me, g),
            back_send.at[g, k],
            back_recv.at[g, k],
            {"seq": peer(k)},
        )

    def back_own(g):
        return pltpu.make_async_copy(
            away(results, me, g), home(d_tokens_ref, me, g), back_recv.at[g, 0]
        )

    moved = (
        (tokens_ref, got_tokens, tokens_send, tokens_recv),
        (d_out_ref, got_d_out, d_out_send, d_out_recv),
    )

    @pl.loop(0, steps)
    def _(g):
        for source, target, send, recv in moved:
            for k in range(1, seq_size):
                spread(source, target, send, recv, g, k).start()
            keep_own(source, target, recv, g).start()

    def arrived(which, g):
        source, target, send, recv = moved[which]
        for k in range(1, seq_size):
            spread(source, target, send, recv, g, k).wait_recv()
        keep_own(source, target, recv, g).wait()

    live_row = jnp.where(order_ref[...] < frames_ref[0], 1.0, 0.0)
    slot_of_row = lax.broadcasted_iota(jnp.int32, (rows, slot_count), 0) // group
    slot = lax.broadcasted_iota(jnp.int32, (rows, slot_count), 1)
    slot_hit = jnp.where(slot_of_row == slot, 1.0, 0.0)
    live_ref[...] = jnp.sum(slot_hit * live_row, axis=-1, keepdims=True)
    key_live = dot(live_row.astype(jnp.bfloat16), slot_hit.astype(jnp.bfloat16), NT)
    patch = lax.broadcasted_iota(jnp.int32, (rows, rows), 0) % group
    key_patch = lax.broadcasted_iota(jnp.int32, (rows, rows), 1) % group
    mask_ref[...] = jnp.where((patch == key_patch) & (key_live > 0.5), 0.0, -1e30)
    for copy in weights:
        copy.wait()
    grad[...] = jnp.zeros_like(grad)

    def pair_copy():
        return remote(
            pair_sent, pair_got, pair_sems.at[0], pair_sems.at[1], {"seq": chip * 2 + 1 - core}
        )

    def row_piece(at, parity):
        start = pl.multiple_of((at * 2 + parity) * row_block, row_block)
        return grad[pl.ds(start, row_block), :]

    def columns_of(value, d):
        return value[:, d * column_block : (d + 1) * column_block]

    @pl.loop(0, steps)
    def _(g):
        arrived(0, g)
        values = got_tokens[g].astype(jnp.float32).reshape(rows, width)
        center = values - jnp.mean(values, axis=-1, keepdims=True)
        inverse = lax.rsqrt(jnp.mean(center * center, axis=-1, keepdims=True) + 1e-06)
        normalized = center * inverse
        joined[...] = dot(normalized.astype(jnp.bfloat16), w_qkv_ref[...]).astype(jnp.bfloat16)
        arrived(1, g)
        masked_wide = got_d_out[g].astype(jnp.float32).reshape(rows, width) * live_ref[...]
        masked = masked_wide.astype(jnp.bfloat16)
        head_grad[...] = dot(masked, w_out_ref[...], NT).astype(jnp.bfloat16)
        attend(joined, head_grad, mask_ref[...], attended, qkv_grad, width, score_scale)
        grad[...] += dot(attended[...], masked, TN)

        @pl.when(g == steps - 1)
        def _():
            @pl.loop(0, chips)
            def _(at):
                value = row_piece(at, 1 - core)
                for d in range(dp_size):
                    pair_sent[d, at] = columns_of(value, d).astype(jnp.bfloat16)

            pair_copy().start()

        normed_grad = dot(qkv_grad[...], w_qkv_ref[...], NT)
        mean_grad = jnp.mean(normed_grad, axis=-1, keepdims=True)
        mean_cross = jnp.mean(normed_grad * normalized, axis=-1, keepdims=True)
        result = masked_wide + inverse * (normed_grad - mean_grad - normalized * mean_cross)
        results[g] = result.reshape(slot_count, group, width).astype(jnp.bfloat16)
        for k in range(1, seq_size):
            back(g, k).start()
        back_own(g).start()

    pair_copy().wait_recv()

    @pl.loop(0, chips)
    def _(at):
        value = row_piece(at, core)
        for d in range(dp_size):
            total = columns_of(value, d) + pair_got[d, at].astype(jnp.float32)
            dp_sent[d, at] = total.astype(jnp.bfloat16)

    def dp_copy(k):
        return remote(
            dp_sent.at[dp_peer(k)],
            dp_got.at[k - 1],
            dp_send.at[k - 1],
            dp_recv.at[k - 1],
            {"dp": dp_peer(k)},
        )

    for k in range(1, dp_size):
        dp_copy(k).start()
    for k in range(1, dp_size):
        dp_copy(k).wait_recv()

    @pl.loop(0, chips)
    def _(at):
        total = dp_sent[my_dp, at].astype(jnp.float32)
        for k in range(1, dp_size):
            total = total + dp_got[k - 1, at].astype(jnp.float32)
        chip_sent[at] = total.astype(jnp.bfloat16)

    def chip_copy(block, slot_at, target):
        return remote(
            chip_sent.at[block],
            chip_got.at[slot_at],
            chip_send.at[slot_at],
            chip_recv.at[slot_at],
            {"seq": target * 2 + core},
        )

    if chips == 4:
        near = chip + 1 - 2 * lax.rem(chip, 2)
        far = lax.rem(chip + 2, chips)
        chip_copies = [
            chip_copy(lax.rem(near + 2, chips), 0, near),
            chip_copy(near, 1, near),
            chip_copy(far, 2, far),
        ]
        chip_copies[0].start()
        chip_copies[1].start()
        chip_copies[0].wait_recv()
        crossing = chip_sent[far].astype(jnp.float32) + chip_got[0].astype(jnp.float32)
        chip_sent[far] = crossing.astype(jnp.bfloat16)
        chip_copies[2].start()
        arriving = (1, 2)
    else:
        chip_copies = []
        for k in range(1, chips):
            target = lax.rem(chip + k, chips)
            chip_copies.append(chip_copy(target, k - 1, target))
            chip_copies[-1].start()
        arriving = range(chips - 1)
    total = chip_sent[chip].astype(jnp.float32)
    for slot_at in arriving:
        chip_copies[slot_at].wait_recv()
        total = total + chip_got[slot_at].astype(jnp.float32)
    final_ref[...] = total

    pair_copy().wait_send()
    for k in range(1, dp_size):
        dp_copy(k).wait_send()
    for copy in chip_copies:
        copy.wait_send()

    @pl.loop(0, steps)
    def _(g):
        for source, target, send, recv in moved:
            for k in range(1, seq_size):
                spread(source, target, send, recv, g, k).wait_send()
        for k in range(1, seq_size):
            back(g, k).wait()
        back_own(g).wait()


def exchange_part(tokens, d_out, frames, frame_order, w_qkv, w_out, slots, seq_size, dp_size):
    row_count, width = tokens.shape
    slot_count = frame_order.shape[1]
    stripe = row_count // slot_count
    steps = stripe // GROUP
    rows = slot_count * GROUP
    chips = seq_size // 2
    tokens = tokens.reshape(slots, row_count // slots, width)
    d_out = d_out.reshape(tokens.shape)
    any_space = pl.BlockSpec(memory_space=pl.ANY)
    vmem = pl.BlockSpec(memory_space=pltpu.VMEM)
    smem = pl.BlockSpec(memory_space=pltpu.SMEM)
    narrow = jnp.bfloat16
    parts = (chips, width // seq_size, width // dp_size)
    crossing = pltpu.SemaphoreType.DMA((steps, seq_size))
    d_tokens, final = pl.pallas_call(
        functools.partial(exchange_kernel, 1.0 / math.sqrt(width // H), seq_size, dp_size),
        in_specs=[any_space, any_space, smem, vmem, any_space, any_space],
        out_specs=[any_space, vmem],
        out_shape=[
            jax.ShapeDtypeStruct(tokens.shape, narrow),
            jax.ShapeDtypeStruct(parts[1:], jnp.float32),
        ],
        scratch_shapes=[
            pltpu.VMEM(w_qkv.shape, narrow),
            pltpu.VMEM(w_out.shape, narrow),
            pltpu.VMEM((steps, slot_count, GROUP, width), narrow),
            pltpu.VMEM((steps, slot_count, GROUP, width), narrow),
            pltpu.VMEM((steps, slot_count, GROUP, width), narrow),
            pltpu.VMEM((rows, 3 * width), narrow),
            pltpu.VMEM((rows, width), narrow),
            pltpu.VMEM((rows, width), narrow),
            pltpu.VMEM((rows, 3 * width), narrow),
            pltpu.VMEM((width, width), jnp.float32),
            pltpu.VMEM((dp_size, *parts), narrow),
            pltpu.VMEM((dp_size, *parts), narrow),
            pltpu.VMEM((dp_size, *parts), narrow),
            pltpu.VMEM((dp_size - 1, *parts), narrow),
            pltpu.VMEM(parts, narrow),
            pltpu.VMEM((chips - 1, *parts[1:]), narrow),
            pltpu.VMEM((rows, 1), jnp.float32),
            pltpu.VMEM((rows, rows), jnp.float32),
            pltpu.SemaphoreType.DMA((2,)),
            crossing,
            crossing,
            crossing,
            crossing,
            crossing,
            crossing,
            pltpu.SemaphoreType.DMA((2,)),
            pltpu.SemaphoreType.DMA((dp_size - 1,)),
            pltpu.SemaphoreType.DMA((dp_size - 1,)),
            pltpu.SemaphoreType.DMA((chips - 1,)),
            pltpu.SemaphoreType.DMA((chips - 1,)),
        ],
        compiler_params=pltpu.CompilerParams(
            collective_id=0, has_side_effects=True, vmem_limit_bytes=60 * 2**20
        ),
    )(tokens, d_out, frames, frame_order, w_qkv, w_out)
    return d_tokens, final


def body(tokens, d_out, frames, frame_order, w_qkv, w_out):
    _, row_count, width = tokens.shape
    seq_size = lax.axis_size("seq")
    slot_count = frame_order.shape[1]
    stripe = row_count // slot_count
    patch_count = row_count * seq_size // slot_count
    slots = max(1, row_count // patch_count)
    piece = row_count // slots // seq_size
    live_slots = (frame_order[0] < frames[0]).astype(jnp.float32)

    dp_size = lax.axis_size("dp")
    if (
        piece == stripe
        and stripe % GROUP == 0
        and seq_size % 2 == 0
        and seq_size > 2
        and dp_size > 1
        and width % (16 * seq_size) == 0
    ):
        d_rows, final_out = exchange_part(
            tokens[0], d_out[0], frames, frame_order, w_qkv, w_out, slots, seq_size, dp_size
        )
        return (d_rows.reshape(tokens.shape), final_out)

    def spread(rows):
        sent = rows.reshape(slots, seq_size, piece, width)
        got = lax.all_to_all(sent, "seq", split_axis=1, concat_axis=0, tiled=True)
        return got.reshape(slot_count, stripe, width)

    d_rows, grad_out = local_part(spread(tokens), spread(d_out), live_slots, w_qkv, w_out)
    back = d_rows.reshape(seq_size * slots, 1, piece, width)
    d_tokens = lax.all_to_all(back, "seq", split_axis=0, concat_axis=1, tiled=True)
    share = lax.psum_scatter(
        grad_out.astype(jnp.bfloat16), "dp", scatter_dimension=1, tiled=True
    ).astype(jnp.float32)
    final_out = lax.psum_scatter(share, "seq", scatter_dimension=0, tiled=True)
    return (d_tokens.reshape(tokens.shape), final_out)


def solution(mesh):
    placed = (P("dp", "seq", None), P("dp", "seq", None), P("dp"), P("dp", None), P(), P())
    return jax.shard_map(
        body,
        mesh=mesh,
        in_specs=placed,
        out_specs=(P("dp", "seq", None), P("seq", "dp")),
        check_vma=False,
    )
```
